32 devices in a mesh: grp: 2 (over x), feed: 16 (over z, y, core).
Axes of the slice: x: 2, y: 2, z: 4, core: 2. Of those that a mesh axis runs over, the one named last changes fastest.
Arguments:
- samples: bfloat16 [32, 256, 65536], P(('grp', 'feed')), parts along dimension 0, may hold values from -6 to 6
- pfb_taps: float32 [4, 8192], replicated, may hold values from -0.03125 to 0.03125
Outputs:
- visibility: float32 [16384, 4096], P(('grp', 'feed')), parts along dimension 0
The draws below stay inside these ranges and needn't reach their ends.
There are 2 independent parts, one for each index of `grp`. The reference program is written for one: setup_inputs(seed, part) draws one part's arguments, and reference() takes and returns one part's arrays. A program takes and returns all parts, laid end to end along the dimension named above; an argument that names none is the same for every part. Nothing has to cross between parts.
All inputs are finite; a program needn't handle non-finite values.
Results may differ from the reference program's by a relative error of at most 0.004.
Values may be sent and summed in bfloat16 or wider, within the bound.
A program may use at most 192 MiB of HBM per device.

```python
import math
import jax
import jax.numpy as jnp
from jax import lax

FEEDS = 2048
NFFT = 8192
TAPS = 4
FIRST_CH = 1536
TIME_BLOCKS = 2
FRAMES_DEV = 8
CH_SLAB = 4
NSPEC = 16
FEED_DEV = 256
N_FEED = 16


def block_levels(rng, dims, shards, least, largest):
    def one(dim, blocks):
        steps = jax.random.uniform(jax.random.fold_in(jax.random.fold_in(rng, 6), dim), (blocks,), jnp.float32, least / len(shards), largest / len(shards))
        return jnp.repeat(jnp.exp(steps), dims[dim] // blocks).reshape((-1,) + (1,) * (len(dims) - dim - 1))

    gain = one(*shards[0])
    for cut in shards[1:]:
        gain = gain * one(*cut)
    return gain


def bell_draw(own_key, dims, spread, bound, shards=(), held_as=jnp.bfloat16):
    entries = jax.random.normal(own_key, dims, jnp.float32) * spread
    if len(shards) > 0:
        entries = block_levels(own_key, dims, shards, -0.22, 0.18) * entries
    return jnp.clip(entries, min=-bound, max=bound).astype(held_as)


def setup_inputs(seed: int = 0, part: int = 0) -> dict:
    splits = jax.random.split(jax.random.key(seed), 3)
    own_keys = jax.random.split(jax.random.fold_in(splits[2], part), 3)
    return {
        "samples": bell_draw(own_keys[0], (N_FEED, FEED_DEV, FRAMES_DEV * NFFT), 1.0, 6.0, ((0, 16),)),
        "pfb_taps": bell_draw(splits[1], (TAPS, NFFT), (TAPS * NFFT) ** -0.5, 0.03125, (), jnp.float32),
    }


def dft_matrix(fft_len, first_channel, channel_count):
    sample_ids = jnp.arange(fft_len, dtype=jnp.int32)
    channel_ids = first_channel + jnp.arange(channel_count, dtype=jnp.int32)
    phase = (sample_ids[:, None] * channel_ids[None, :]) % fft_len
    angle = phase.astype(jnp.float32) * (2.0 * math.pi / fft_len)
    return jnp.concatenate([jnp.cos(angle), -jnp.sin(angle)], axis=1)


def reference(samples, pfb_taps):
    blocks = samples.reshape(TIME_BLOCKS, N_FEED // TIME_BLOCKS, FEED_DEV, FRAMES_DEV, NFFT)
    frames = jnp.transpose(blocks, (1, 2, 0, 3, 4)).reshape(FEEDS // FEED_DEV, FEED_DEV, NSPEC, NFFT)
    dft_table = dft_matrix(NFFT, FIRST_CH, CH_SLAB)

    def transform(part_frames):
        padded = jnp.concatenate([jnp.zeros((FEED_DEV, TAPS - 1, NFFT), part_frames.dtype), part_frames], axis=1)
        filtered = jnp.zeros((FEED_DEV, NSPEC, NFFT), jnp.float32)
        for tap_index in range(TAPS):
            filtered = filtered + padded[:, tap_index:tap_index + NSPEC].astype(jnp.float32) * pfb_taps[tap_index]
        spectra = jnp.dot(filtered.reshape(FEED_DEV * NSPEC, NFFT), dft_table, precision=lax.Precision.HIGHEST, preferred_element_type=jnp.float32)
        return spectra.astype(jnp.bfloat16).reshape(FEED_DEV, NSPEC, 2 * CH_SLAB)

    spectra = lax.map(transform, frames).reshape(FEEDS, NSPEC, 2 * CH_SLAB)
    real_all = jnp.moveaxis(spectra[:, :, :CH_SLAB], 2, 0)
    imag_all = jnp.moveaxis(spectra[:, :, CH_SLAB:], 2, 0)

    def correlate(pair):
        real_part, imag_part = pair
        all_feeds = jnp.concatenate([real_part, imag_part], axis=1)
        right_matrix = jnp.concatenate([all_feeds, jnp.concatenate([-imag_part, real_part], axis=1)], axis=0).T
        return jnp.dot(all_feeds, right_matrix, preferred_element_type=jnp.float32) * (1.0 / NSPEC)

    visibility = lax.map(correlate, (real_all, imag_all))
    return visibility.reshape(CH_SLAB * FEEDS, 2 * FEEDS)
```

```python
import functools
import math

import jax
import jax.numpy as jnp
import numpy as np
from jax import lax
from jax.experimental import pallas as pl
from jax.experimental.pallas import tpu as pltpu
from jax.sharding import PartitionSpec as P

FIRST_CH = 1536
TIME_BLOCKS = 2
ROWS_DEV = 512
PARTS = 3
CHUNKS = 4


def dft_rows(fft_len, channels):
    phase = (np.arange(fft_len)[None, :] * (FIRST_CH + np.arange(channels))[:, None]) % fft_len
    angle = phase * (2.0 * math.pi / fft_len)
    return np.concatenate([np.cos(angle), -np.sin(angle)], axis=0).astype(np.float32)


def channelize_kernel(
    devices, samples_ref, taps_ref, table_ref, out_ref,
    frames_buf, taps_buf, table_buf, w_buf, g_buf, spec_buf, msg_buf, spill_out, spill_in,
    load_sems, aux_sems, spill_sems, send_sems, recv_sems, own_sem,
):
    me = lax.axis_index("feed")
    span = devices // TIME_BLOCKS
    frame_count, feeds, fft_len = frames_buf.shape
    tap_count = taps_buf.shape[0]
    cols = table_buf.shape[0]
    channels = cols // 2
    owners = devices // channels
    edge = tap_count - 1
    chunk = fft_len // CHUNKS
    early = frame_count - edge

    aux = [
        pltpu.make_async_copy(taps_ref, taps_buf, aux_sems.at[0]),
        pltpu.make_async_copy(table_ref, table_buf, aux_sems.at[1]),
    ]
    for copy in aux:
        copy.start()

    def load(frame, part):
        start = pl.multiple_of(frame * fft_len + part * chunk, 128)
        return pltpu.make_async_copy(
            samples_ref.at[0, :, pl.ds(start, chunk)],
            frames_buf.at[frame, :, pl.ds(part * chunk, chunk)],
            load_sems.at[frame * CHUNKS + part],
        )

    def start_frame(step, carry):
        frame = lax.rem(step + early, frame_count)
        for part in range(CHUNKS):
            load(frame, part).start()
        return carry

    lax.fori_loop(0, frame_count, start_frame, 0)

    barrier = pltpu.get_barrier_semaphore()

    def greet(step, carry):
        peer = lax.rem(me + step, devices)
        pl.semaphore_signal(barrier, inc=1, device_id={"feed": peer}, device_id_type=pl.DeviceIdType.MESH)
        return carry

    lax.fori_loop(1, devices, greet, 0)

    for copy in aux:
        copy.wait()
    for tap in range(tap_count):
        rest = taps_buf[tap : tap + 1, :] * table_buf[...]
        for part in range(PARTS):
            piece = rest.astype(jnp.bfloat16)
            row = (part * tap_count + tap) * cols
            w_buf[row : row + cols, :] = piece
            rest = rest - piece.astype(jnp.float32)

    pl.semaphore_wait(barrier, devices - 1)

    def do_frame(frame, carry):
        total = None
        for part in range(CHUNKS):
            load(frame, part).wait()
            columns = slice(part * chunk, (part + 1) * chunk)
            product = lax.dot_general(
                w_buf[:, columns], frames_buf[frame, :, columns],
                (((1,), (1,)), ((), ())), preferred_element_type=jnp.float32,
            )
            total = product if total is None else total + product
        rows = tap_count * cols
        summed = total[:rows]
        for part in range(1, PARTS):
            summed = summed + total[part * rows : (part + 1) * rows]
        g_buf[frame] = summed
        return carry

    lax.fori_loop(early, frame_count, do_frame, 0)

    for later in range(edge):
        total = g_buf[early + later, 0:cols, :]
        for tap in range(1, edge - later):
            total = total + g_buf[early + later + tap, tap * cols : (tap + 1) * cols, :]
        spill_out[later] = total
    spill = pltpu.make_async_remote_copy(
        src_ref=spill_out, dst_ref=spill_in, send_sem=spill_sems.at[0], recv_sem=spill_sems.at[1],
        device_id={"feed": lax.rem(me + span, devices)}, device_id_type=pl.DeviceIdType.MESH,
    )

    @pl.when(me < span)
    def _():
        spill.start()
        spill_in[...] = jnp.zeros_like(spill_in)

    lax.fori_loop(0, early, do_frame, 0)

    @pl.when(me < span)
    def _():
        spill.wait_send()

    @pl.when(me >= span)
    def _():
        spill.wait_recv()

    for time in range(frame_count):
        total = spill_in[time] if time < edge else None
        for tap in range(tap_count):
            frame = time - edge + tap
            if frame >= 0:
                term = g_buf[frame, tap * cols : (tap + 1) * cols, :]
                total = term if total is None else total + term
        spec_buf[:, time, :] = total
    for channel in range(channels):
        msg_buf[channel] = jnp.concatenate(
            [spec_buf[channel], spec_buf[channels + channel]], axis=0
        ).astype(jnp.bfloat16)

    own = pltpu.make_async_copy(msg_buf.at[me // owners], out_ref.at[me], own_sem)

    def message(peer, slot, source):
        return pltpu.make_async_remote_copy(
            src_ref=msg_buf.at[peer // owners], dst_ref=out_ref.at[source],
            send_sem=send_sems.at[slot], recv_sem=recv_sems.at[slot],
            device_id={"feed": peer}, device_id_type=pl.DeviceIdType.MESH,
        )

    def send(step, carry):
        message(lax.rem(me + step, devices), step, me).start()
        return carry

    def finish(step, carry):
        copy = message(lax.rem(me + step, devices), step, lax.rem(me + devices - step, devices))
        copy.wait_send()
        copy.wait_recv()
        return carry

    lax.fori_loop(1, devices, send, 0)
    own.start()
    lax.fori_loop(1, devices, finish, 0)
    own.wait()


def correlate_kernel(devices, gathered_ref, out_ref, right_buf):
    _, depth, feeds = gathered_ref.shape
    half = depth // 2
    span = devices // TIME_BLOCKS
    total_feeds = span * feeds
    owners = total_feeds // ROWS_DEV
    rows = out_ref.shape[0]
    me = lax.axis_index("feed")
    spectra_count = TIME_BLOCKS * half

    @pl.when(pl.program_id(0) == 0)
    def _():
        for block in range(TIME_BLOCKS):
            for group in range(span):
                piece = gathered_ref[block * span + group]
                wide = piece.astype(jnp.float32)
                turned = jnp.concatenate([-wide[half:], wide[:half]], axis=0).astype(jnp.bfloat16)
                lines = slice(block * depth, (block + 1) * depth)
                right_buf[lines, group * feeds : (group + 1) * feeds] = piece
                right_buf[lines, total_feeds + group * feeds : total_feeds + (group + 1) * feeds] = turned

    start = pl.multiple_of(lax.rem(me, owners) * ROWS_DEV + pl.program_id(0) * rows, 128)
    left = right_buf[:, pl.ds(start, rows)]
    out_ref[...] = lax.dot_general(
        left, right_buf[...], (((0,), (0,)), ((), ())), preferred_element_type=jnp.float32
    ) * (1.0 / spectra_count)


def body(samples, pfb_taps):
    feeds = samples.shape[1]
    tap_count, fft_len = pfb_taps.shape
    frame_count = samples.shape[2] // fft_len
    devices = lax.axis_size("feed")
    total_feeds = feeds * (devices // TIME_BLOCKS)
    channels = devices * ROWS_DEV // total_feeds
    cols = 2 * channels
    edge = tap_count - 1
    table = jnp.asarray(dft_rows(fft_len, channels))
    anywhere = pl.BlockSpec(memory_space=pl.ANY)
    gathered = pl.pallas_call(
        functools.partial(channelize_kernel, devices),
        out_shape=jax.ShapeDtypeStruct((devices, 2 * frame_count, feeds), jnp.bfloat16),
        in_specs=[anywhere] * 3,
        out_specs=anywhere,
        scratch_shapes=[
            pltpu.VMEM((frame_count, feeds, fft_len), jnp.bfloat16),
            pltpu.VMEM((tap_count, fft_len), jnp.float32),
            pltpu.VMEM((cols, fft_len), jnp.float32),
            pltpu.VMEM((PARTS * tap_count * cols, fft_len), jnp.bfloat16),
            pltpu.VMEM((frame_count, tap_count * cols, feeds), jnp.float32),
            pltpu.VMEM((cols, frame_count, feeds), jnp.float32),
            pltpu.VMEM((channels, 2 * frame_count, feeds), jnp.bfloat16),
            pltpu.VMEM((edge, cols, feeds), jnp.float32),
            pltpu.VMEM((edge, cols, feeds), jnp.float32),
            pltpu.SemaphoreType.DMA((frame_count * CHUNKS,)),
            pltpu.SemaphoreType.DMA((2,)),
            pltpu.SemaphoreType.DMA((2,)),
            pltpu.SemaphoreType.DMA((devices,)),
            pltpu.SemaphoreType.DMA((devices,)),
            pltpu.SemaphoreType.DMA,
        ],
        compiler_params=pltpu.CompilerParams(
            collective_id=0, has_side_effects=True, vmem_limit_bytes=56 * 2**20
        ),
        name="channelize",
    )(samples, pfb_taps, table)
    block_rows = ROWS_DEV // 4
    return pl.pallas_call(
        functools.partial(correlate_kernel, devices),
        out_shape=jax.ShapeDtypeStruct((ROWS_DEV, 2 * total_feeds), jnp.float32),
        grid=(ROWS_DEV // block_rows,),
        in_specs=[pl.BlockSpec(gathered.shape, lambda i: (0, 0, 0))],
        out_specs=pl.BlockSpec((block_rows, 2 * total_feeds), lambda i: (i, 0)),
        scratch_shapes=[pltpu.VMEM((TIME_BLOCKS * 2 * frame_count, 2 * total_feeds), jnp.bfloat16)],
        compiler_params=pltpu.CompilerParams(vmem_limit_bytes=32 * 2**20),
        name="correlate",
    )(gathered)


def solution(mesh):
    placed = (P(("grp", "feed"), None, None), P())
    return jax.shard_map(
        body, mesh=mesh, in_specs=placed, out_specs=P(("grp", "feed"), None), check_vma=False
    )
```

```python
import functools
import math

import jax
import jax.numpy as jnp
import numpy as np
from jax import lax
from jax.experimental import pallas as pl
from jax.experimental.pallas import tpu as pltpu
from jax.sharding import PartitionSpec as P

FIRST_CH = 1536
TIME_BLOCKS = 2
ROWS_DEV = 512
PARTS = 3
CHUNKS = 8
GROUPS = 2


def dft_rows(fft_len, channels):
    phase = (np.arange(fft_len)[None, :] * (FIRST_CH + np.arange(channels))[:, None]) % fft_len
    angle = phase * (2.0 * math.pi / fft_len)
    return np.concatenate([np.cos(angle), -np.sin(angle)], axis=0).astype(np.float32)


def channelize_kernel(
    devices, samples_ref, taps_ref, table_ref, out_ref,
    frames_buf, taps_buf, table_buf, w_buf, g_buf, spec_buf, msg_buf, spill_out, spill_in, acc_buf,
    load_sems, aux_sems, spill_sems, send_sems, recv_sems, own_sem,
):
    me = lax.axis_index("feed")
    span = devices // TIME_BLOCKS
    frame_count, feeds, fft_len = frames_buf.shape
    tap_count = taps_buf.shape[0]
    cols = table_buf.shape[0]
    channels = cols // 2
    owners = devices // channels
    edge = tap_count - 1
    chunk = fft_len // CHUNKS
    early = frame_count - edge

    aux = [
        pltpu.make_async_copy(taps_ref, taps_buf, aux_sems.at[0]),
        pltpu.make_async_copy(table_ref, table_buf, aux_sems.at[1]),
    ]
    for copy in aux:
        copy.start()

    group_frames = frame_count // GROUPS

    def load(frame, part):
        start = pl.multiple_of(frame * fft_len + part * chunk, 128)
        here = pl.multiple_of(part * chunk, 128)
        return pltpu.make_async_copy(
            samples_ref.at[0, :, pl.ds(start, chunk)],
            frames_buf.at[frame, :, pl.ds(here, chunk)],
            load_sems.at[frame * CHUNKS + part],
        )

    def start_part(step, carry):
        group = GROUPS - 1 - step // CHUNKS
        for inner in range(group_frames):
            load(group * group_frames + inner, lax.rem(step, CHUNKS)).start()
        return carry

    lax.fori_loop(0, GROUPS * CHUNKS, start_part, 0)

    barrier = pltpu.get_barrier_semaphore()

    def greet(step, carry):
        peer = lax.rem(me + step, devices)
        pl.semaphore_signal(barrier, inc=1, device_id={"feed": peer}, device_id_type=pl.DeviceIdType.MESH)
        return carry

    lax.fori_loop(1, devices, greet, 0)

    for copy in aux:
        copy.wait()
    def build(part):
        for block in range(chunk // 256):
            lines = pl.ds(part * chunk + block * 256, 256)
            pieces = [[] for _ in range(PARTS)]
            for tap in range(tap_count):
                rest = taps_buf[tap : tap + 1, lines] * table_buf[:, lines]
                for index in range(PARTS):
                    piece = rest.astype(jnp.bfloat16).astype(jnp.float32)
                    pieces[index].append(piece)
                    rest = rest - piece
            w_buf[lines, :] = jnp.concatenate(sum(pieces, []), axis=0).T.astype(jnp.bfloat16)

    def do_part(group, part, first):
        begin = group * group_frames
        for inner in range(group_frames):
            load(begin + inner, part).wait()
        lines = pl.ds(part * chunk if isinstance(part, int) else pl.multiple_of(part * chunk, 128), chunk)
        block = frames_buf[begin : begin + group_frames, :, lines]
        product = jnp.dot(
            block.reshape(group_frames * feeds, chunk), w_buf[lines, :],
            preferred_element_type=jnp.float32,
        )
        acc_buf[...] = product if first else acc_buf[...] + product

    def end_group(group):
        rows = tap_count * cols
        for inner in range(group_frames):
            total = acc_buf[inner * feeds : (inner + 1) * feeds, :].T
            summed = total[:rows]
            for index in range(1, PARTS):
                summed = summed + total[index * rows : (index + 1) * rows]
            g_buf[group * group_frames + inner] = summed

    build(0)
    for part in range(CHUNKS):
        if part + 1 < CHUNKS:
            build(part + 1)
        do_part(GROUPS - 1, part, part == 0)
    end_group(GROUPS - 1)
    pl.semaphore_wait(barrier, devices - 1)

    for later in range(edge):
        total = g_buf[early + later, 0:cols, :]
        for tap in range(1, edge - later):
            total = total + g_buf[early + later + tap, tap * cols : (tap + 1) * cols, :]
        spill_out[later] = total
    spill = pltpu.make_async_remote_copy(
        src_ref=spill_out, dst_ref=spill_in, send_sem=spill_sems.at[0], recv_sem=spill_sems.at[1],
        device_id={"feed": lax.rem(me + span, devices)}, device_id_type=pl.DeviceIdType.MESH,
    )

    @pl.when(me < span)
    def _():
        spill.start()
        spill_in[...] = jnp.zeros_like(spill_in)

    for group in reversed(range(GROUPS - 1)):
        do_part(group, 0, True)

        def more(part, carry):
            do_part(group, part, False)
            return carry

        lax.fori_loop(1, CHUNKS, more, 0)
        end_group(group)

    @pl.when(me < span)
    def _():
        spill.wait_send()

    @pl.when(me >= span)
    def _():
        spill.wait_recv()

    for time in range(frame_count):
        total = spill_in[time] if time < edge else None
        for tap in range(tap_count):
            frame = time - edge + tap
            if frame >= 0:
                term = g_buf[frame, tap * cols : (tap + 1) * cols, :]
                total = term if total is None else total + term
        spec_buf[:, time, :] = total
    for channel in range(channels):
        msg_buf[channel] = jnp.concatenate(
            [spec_buf[channel], spec_buf[channels + channel]], axis=0
        ).astype(jnp.bfloat16)

    own = pltpu.make_async_copy(msg_buf.at[me // owners], out_ref.at[me], own_sem)

    def message(peer, slot, source):
        return pltpu.make_async_remote_copy(
            src_ref=msg_buf.at[peer // owners], dst_ref=out_ref.at[source],
            send_sem=send_sems.at[slot], recv_sem=recv_sems.at[slot],
            device_id={"feed": peer}, device_id_type=pl.DeviceIdType.MESH,
        )

    def send(step, carry):
        message(lax.rem(me + step, devices), step, me).start()
        return carry

    def finish(step, carry):
        copy = message(lax.rem(me + step, devices), step, lax.rem(me + devices - step, devices))
        copy.wait_send()
        copy.wait_recv()
        return carry

    lax.fori_loop(1, devices, send, 0)
    own.start()
    lax.fori_loop(1, devices, finish, 0)
    own.wait()


def correlate_kernel(devices, gathered_ref, out_ref, right_buf):
    _, depth, feeds = gathered_ref.shape
    half = depth // 2
    span = devices // TIME_BLOCKS
    total_feeds = span * feeds
    owners = total_feeds // ROWS_DEV
    rows = out_ref.shape[0]
    me = lax.axis_index("feed")
    spectra_count = TIME_BLOCKS * half

    @pl.when(pl.program_id(0) == 0)
    def _():
        for block in range(TIME_BLOCKS):
            for group in range(span):
                piece = gathered_ref[block * span + group]
                wide = piece.astype(jnp.float32)
                turned = jnp.concatenate([-wide[half:], wide[:half]], axis=0).astype(jnp.bfloat16)
                lines = slice(block * depth, (block + 1) * depth)
                right_buf[lines, group * feeds : (group + 1) * feeds] = piece
                right_buf[lines, total_feeds + group * feeds : total_feeds + (group + 1) * feeds] = turned

    start = pl.multiple_of(lax.rem(me, owners) * ROWS_DEV + pl.program_id(0) * rows, 128)
    left = right_buf[:, pl.ds(start, rows)]
    out_ref[...] = lax.dot_general(
        left, right_buf[...], (((0,), (0,)), ((), ())), preferred_element_type=jnp.float32
    ) * (1.0 / spectra_count)


def body(samples, pfb_taps):
    feeds = samples.shape[1]
    tap_count, fft_len = pfb_taps.shape
    frame_count = samples.shape[2] // fft_len
    devices = lax.axis_size("feed")
    total_feeds = feeds * (devices // TIME_BLOCKS)
    channels = devices * ROWS_DEV // total_feeds
    cols = 2 * channels
    edge = tap_count - 1
    table = jnp.asarray(dft_rows(fft_len, channels))
    anywhere = pl.BlockSpec(memory_space=pl.ANY)
    gathered = pl.pallas_call(
        functools.partial(channelize_kernel, devices),
        out_shape=jax.ShapeDtypeStruct((devices, 2 * frame_count, feeds), jnp.bfloat16),
        in_specs=[anywhere] * 3,
        out_specs=anywhere,
        scratch_shapes=[
            pltpu.VMEM((frame_count, feeds, fft_len), jnp.bfloat16),
            pltpu.VMEM((tap_count, fft_len), jnp.float32),
            pltpu.VMEM((cols, fft_len), jnp.float32),
            pltpu.VMEM((fft_len, PARTS * tap_count * cols), jnp.bfloat16),
            pltpu.VMEM((frame_count, tap_count * cols, feeds), jnp.float32),
            pltpu.VMEM((cols, frame_count, feeds), jnp.float32),
            pltpu.VMEM((channels, 2 * frame_count, feeds), jnp.bfloat16),
            pltpu.VMEM((edge, cols, feeds), jnp.float32),
            pltpu.VMEM((edge, cols, feeds), jnp.float32),
            pltpu.VMEM((frame_count // GROUPS * feeds, PARTS * tap_count * cols), jnp.float32),
            pltpu.SemaphoreType.DMA((frame_count * CHUNKS,)),
            pltpu.SemaphoreType.DMA((2,)),
            pltpu.SemaphoreType.DMA((2,)),
            pltpu.SemaphoreType.DMA((devices,)),
            pltpu.SemaphoreType.DMA((devices,)),
            pltpu.SemaphoreType.DMA,
        ],
        compiler_params=pltpu.CompilerParams(
            collective_id=0, has_side_effects=True, vmem_limit_bytes=56 * 2**20
        ),
        name="channelize",
    )(samples, pfb_taps, table)
    block_rows = ROWS_DEV // 4
    return pl.pallas_call(
        functools.partial(correlate_kernel, devices),
        out_shape=jax.ShapeDtypeStruct((ROWS_DEV, 2 * total_feeds), jnp.float32),
        grid=(ROWS_DEV // block_rows,),
        in_specs=[pl.BlockSpec(gathered.shape, lambda i: (0, 0, 0))],
        out_specs=pl.BlockSpec((block_rows, 2 * total_feeds), lambda i: (i, 0)),
        scratch_shapes=[pltpu.VMEM((TIME_BLOCKS * 2 * frame_count, 2 * total_feeds), jnp.bfloat16)],
        compiler_params=pltpu.CompilerParams(vmem_limit_bytes=32 * 2**20),
        name="correlate",
    )(gathered)


def solution(mesh):
    placed = (P(("grp", "feed"), None, None), P())
    return jax.shard_map(
        body, mesh=mesh, in_specs=placed, out_specs=P(("grp", "feed"), None), check_vma=False
    )
```

```python
import functools
import math

import jax
import jax.numpy as jnp
import numpy as np
from jax import lax
from jax.experimental import pallas as pl
from jax.experimental.pallas import tpu as pltpu
from jax.sharding import PartitionSpec as P

FIRST_CH = 1536
TIME_BLOCKS = 2
ROWS_DEV = 512
PARTS = 3
CHUNKS = 8
GROUPS = 2


def dft_rows(fft_len, channels):
    phase = (np.arange(fft_len)[None, :] * (FIRST_CH + np.arange(channels))[:, None]) % fft_len
    angle = phase * (2.0 * math.pi / fft_len)
    return np.concatenate([np.cos(angle), -np.sin(angle)], axis=0).astype(np.float32)


def channelize_kernel(
    devices, samples_ref, taps_ref, table_ref, out_ref,
    frames_buf, taps_buf, table_buf, w_buf, g_buf, spec_buf, msg_buf, spill_out, spill_in, acc_buf,
    load_sems, aux_sems, spill_sems, send_sems, recv_sems, own_sem,
):
    me = lax.axis_index("feed")
    span = devices // TIME_BLOCKS
    frame_count, feeds, fft_len = frames_buf.shape
    tap_count = taps_buf.shape[0]
    cols = table_buf.shape[0]
    channels = cols // 2
    owners = devices // channels
    edge = tap_count - 1
    chunk = fft_len // CHUNKS
    early = frame_count - edge

    aux = [
        pltpu.make_async_copy(taps_ref, taps_buf, aux_sems.at[0]),
        pltpu.make_async_copy(table_ref, table_buf, aux_sems.at[1]),
    ]
    for copy in aux:
        copy.start()

    group_frames = frame_count // GROUPS

    def load(frame, part):
        start = pl.multiple_of(frame * fft_len + part * chunk, 128)
        here = pl.multiple_of(part * chunk, 128)
        return pltpu.make_async_copy(
            samples_ref.at[0, :, pl.ds(start, chunk)],
            frames_buf.at[frame, :, pl.ds(here, chunk)],
            load_sems.at[frame * CHUNKS + part],
        )

    def start_part(step, carry):
        group = GROUPS - 1 - step // CHUNKS
        for inner in range(group_frames):
            load(group * group_frames + inner, lax.rem(step, CHUNKS)).start()
        return carry

    lax.fori_loop(0, GROUPS * CHUNKS, start_part, 0)

    barrier = pltpu.get_barrier_semaphore()

    def greet(step, carry):
        peer = lax.rem(me + step, devices)
        pl.semaphore_signal(barrier, inc=1, device_id={"feed": peer}, device_id_type=pl.DeviceIdType.MESH)
        return carry

    lax.fori_loop(1, devices, greet, 0)

    for copy in aux:
        copy.wait()
    def build(part):
        for block in range(chunk // 256):
            lines = pl.ds(part * chunk + block * 256, 256)
            pieces = [[] for _ in range(PARTS)]
            for tap in range(tap_count):
                rest = taps_buf[tap : tap + 1, lines] * table_buf[:, lines]
                for index in range(PARTS):
                    piece = rest.astype(jnp.bfloat16).astype(jnp.float32)
                    pieces[index].append(piece)
                    rest = rest - piece
            w_buf[lines, :] = jnp.concatenate(sum(pieces, []), axis=0).T.astype(jnp.bfloat16)

    def do_part(group, part, first):
        begin = group * group_frames
        for inner in range(group_frames):
            load(begin + inner, part).wait()
        lines = pl.ds(part * chunk if isinstance(part, int) else pl.multiple_of(part * chunk, 128), chunk)
        block = frames_buf[begin : begin + group_frames, :, lines]
        product = jnp.dot(
            block.reshape(group_frames * feeds, chunk), w_buf[lines, :],
            preferred_element_type=jnp.float32,
        )
        acc_buf[...] = product if first else acc_buf[...] + product

    def end_group(group):
        rows = tap_count * cols
        for inner in range(group_frames):
            total = acc_buf[inner * feeds : (inner + 1) * feeds, :].T
            summed = total[:rows]
            for index in range(1, PARTS):
                summed = summed + total[index * rows : (index + 1) * rows]
            g_buf[group * group_frames + inner] = summed

    build(0)
    for part in range(CHUNKS):
        if part + 1 < CHUNKS:
            build(part + 1)
        do_part(GROUPS - 1, part, part == 0)
    end_group(GROUPS - 1)
    pl.semaphore_wait(barrier, devices - 1)

    for later in range(edge):
        total = g_buf[early + later, 0:cols, :]
        for tap in range(1, edge - later):
            total = total + g_buf[early + later + tap, tap * cols : (tap + 1) * cols, :]
        spill_out[later] = total
    spill = pltpu.make_async_remote_copy(
        src_ref=spill_out, dst_ref=spill_in, send_sem=spill_sems.at[0], recv_sem=spill_sems.at[1],
        device_id={"feed": lax.rem(me + span, devices)}, device_id_type=pl.DeviceIdType.MESH,
    )

    @pl.when(me < span)
    def _():
        spill.start()
        spill_in[...] = jnp.zeros_like(spill_in)

    for group in reversed(range(GROUPS - 1)):
        do_part(group, 0, True)

        def more(part, carry):
            do_part(group, part, False)
            return carry

        lax.fori_loop(1, CHUNKS, more, 0)
        end_group(group)

    @pl.when(me < span)
    def _():
        spill.wait_send()

    @pl.when(me >= span)
    def _():
        spill.wait_recv()

    for time in range(frame_count):
        total = spill_in[time] if time < edge else None
        for tap in range(tap_count):
            frame = time - edge + tap
            if frame >= 0:
                term = g_buf[frame, tap * cols : (tap + 1) * cols, :]
                total = term if total is None else total + term
        spec_buf[:, time, :] = total
    for channel in range(channels):
        msg_buf[channel] = jnp.concatenate(
            [spec_buf[channel], spec_buf[channels + channel]], axis=0
        ).astype(jnp.bfloat16)

    own = pltpu.make_async_copy(msg_buf.at[me // owners], out_ref.at[me], own_sem)

    def message(peer, slot, source):
        return pltpu.make_async_remote_copy(
            src_ref=msg_buf.at[peer // owners], dst_ref=out_ref.at[source],
            send_sem=send_sems.at[slot], recv_sem=recv_sems.at[slot],
            device_id={"feed": peer}, device_id_type=pl.DeviceIdType.MESH,
        )

    def send(step, carry):
        message(lax.rem(me + step, devices), step, me).start()
        return carry

    def finish(step, carry):
        copy = message(lax.rem(me + step, devices), step, lax.rem(me + devices - step, devices))
        copy.wait_send()
        copy.wait_recv()
        return carry

    lax.fori_loop(1, devices, send, 0)
    own.start()
    lax.fori_loop(1, devices, finish, 0)
    own.wait()


def correlate_kernel(devices, gathered_ref, out_ref, right_buf):
    _, depth, feeds = gathered_ref.shape
    half = depth // 2
    span = devices // TIME_BLOCKS
    total_feeds = span * feeds
    owners = total_feeds // ROWS_DEV
    rows = out_ref.shape[0]
    me = lax.axis_index("feed")
    spectra_count = TIME_BLOCKS * half

    @pl.when(pl.program_id(0) == 0)
    def _():
        for block in range(TIME_BLOCKS):
            for group in range(span):
                right_buf[
                    block * depth : (block + 1) * depth, group * feeds : (group + 1) * feeds
                ] = gathered_ref[block * span + group]

    start = pl.multiple_of(lax.rem(me, owners) * ROWS_DEV + pl.program_id(0) * rows, 128)
    left = right_buf[:, pl.ds(start, rows)]
    wide = left.astype(jnp.float32)
    turned = []
    for block in range(TIME_BLOCKS):
        middle = block * depth + half
        turned += [wide[middle : middle + half], -wide[middle - half : middle]]
    both = jnp.concatenate([left, jnp.concatenate(turned, axis=0).astype(jnp.bfloat16)], axis=1)
    product = lax.dot_general(
        both, right_buf[...], (((0,), (0,)), ((), ())), preferred_element_type=jnp.float32
    ) * (1.0 / spectra_count)
    out_ref[:, :total_feeds] = product[:rows]
    out_ref[:, total_feeds:] = product[rows:]


def body(samples, pfb_taps):
    feeds = samples.shape[1]
    tap_count, fft_len = pfb_taps.shape
    frame_count = samples.shape[2] // fft_len
    devices = lax.axis_size("feed")
    total_feeds = feeds * (devices // TIME_BLOCKS)
    channels = devices * ROWS_DEV // total_feeds
    cols = 2 * channels
    edge = tap_count - 1
    table = jnp.asarray(dft_rows(fft_len, channels))
    anywhere = pl.BlockSpec(memory_space=pl.ANY)
    gathered = pl.pallas_call(
        functools.partial(channelize_kernel, devices),
        out_shape=pltpu.VMEM((devices, 2 * frame_count, feeds), jnp.bfloat16),
        in_specs=[anywhere] * 3,
        out_specs=pl.BlockSpec(memory_space=pltpu.VMEM),
        scratch_shapes=[
            pltpu.VMEM((frame_count, feeds, fft_len), jnp.bfloat16),
            pltpu.VMEM((tap_count, fft_len), jnp.float32),
            pltpu.VMEM((cols, fft_len), jnp.float32),
            pltpu.VMEM((fft_len, PARTS * tap_count * cols), jnp.bfloat16),
            pltpu.VMEM((frame_count, tap_count * cols, feeds), jnp.float32),
            pltpu.VMEM((cols, frame_count, feeds), jnp.float32),
            pltpu.VMEM((channels, 2 * frame_count, feeds), jnp.bfloat16),
            pltpu.VMEM((edge, cols, feeds), jnp.float32),
            pltpu.VMEM((edge, cols, feeds), jnp.float32),
            pltpu.VMEM((frame_count // GROUPS * feeds, PARTS * tap_count * cols), jnp.float32),
            pltpu.SemaphoreType.DMA((frame_count * CHUNKS,)),
            pltpu.SemaphoreType.DMA((2,)),
            pltpu.SemaphoreType.DMA((2,)),
            pltpu.SemaphoreType.DMA((devices,)),
            pltpu.SemaphoreType.DMA((devices,)),
            pltpu.SemaphoreType.DMA,
        ],
        compiler_params=pltpu.CompilerParams(
            collective_id=0, has_side_effects=True, vmem_limit_bytes=56 * 2**20
        ),
        name="channelize",
    )(samples, pfb_taps, table)
    block_rows = ROWS_DEV // 4
    return pl.pallas_call(
        functools.partial(correlate_kernel, devices),
        out_shape=jax.ShapeDtypeStruct((ROWS_DEV, 2 * total_feeds), jnp.float32),
        grid=(ROWS_DEV // block_rows,),
        in_specs=[pl.BlockSpec(gathered.shape, lambda i: (0, 0, 0))],
        out_specs=pl.BlockSpec((block_rows, 2 * total_feeds), lambda i: (i, 0)),
        scratch_shapes=[pltpu.VMEM((TIME_BLOCKS * 2 * frame_count, total_feeds), jnp.bfloat16)],
        compiler_params=pltpu.CompilerParams(vmem_limit_bytes=32 * 2**20),
        name="correlate",
    )(gathered)


def solution(mesh):
    placed = (P(("grp", "feed"), None, None), P())
    return jax.shard_map(
        body, mesh=mesh, in_specs=placed, out_specs=P(("grp", "feed"), None), check_vma=False
    )
```
